512 devices in a mesh: sub: 16 (over z, core), tile: 32 (over y, x).
Axes of the slice: x: 4, y: 8, z: 8, core: 2. Of those that a mesh axis runs over, the one named last changes fastest.
Arguments:
- echoes: float32 [32, 32, 128], P('sub', 'tile'), may hold values from -6 to 6
- pulse_offset: float32 [32, 32], P('sub', 'tile'), may hold values from 0 to 1
- range_gates: int32 [32, 32, 64], P('sub', 'tile'), may hold values from 0 to 511
- visible: int32 [32, 256], P('sub', 'tile'), may hold values 0 or 1
Outputs:
- images: float32 [32, 256, 128, 256], P('sub', 'tile')
- peak: float32 [256, 128, 128], P('tile', 'sub')
The draws below stay inside these ranges and needn't reach their ends.
All inputs are finite; a program needn't handle non-finite values. No bound on the sum of `visible` on one device may be relied on, other than what follows from the above.
Results may differ from the reference program's by a relative error of at most 0.0037.
Values sent between devices are 32-bit elements; how exact they have to be, the bound alone decides.
No kernel may reach another device: no remote copies, remote signals or barrier semaphores. Data moves between devices by JAX's collectives and lax.ppermute only.
A program may use at most 64 MiB of HBM per device.

```python
import math
import jax
import jax.numpy as jnp
from jax import lax

PULSE_H = 32
FREQS = 64
PIX = 128
GATES = 512
HALVES = 32
TILES = 256


def plant(drawn, key, least, high):
    shape = drawn.shape
    place = [jax.random.randint(jax.random.fold_in(key, axis), (), 0, shape[axis]) for axis in range(len(shape))]
    drawn = drawn.at[tuple(place)].set(least)
    longest = shape.index(max(shape))
    place[longest] = (place[longest] + 1) % shape[longest]
    return drawn.at[tuple(place)].set(high)


def block_scale(own_key, shape, split, least, high):
    def one(position, blocks):
        steps = jax.random.uniform(jax.random.fold_in(jax.random.fold_in(own_key, 6), position), (blocks,), jnp.float32, least / len(split), high / len(split))
        return jnp.repeat(jnp.exp(steps), shape[position] // blocks).reshape((-1,) + (1,) * (len(shape) - position - 1))

    level = one(*split[0])
    for cut in split[1:]:
        level = level * one(*cut)
    return level


def bell_draw(rng, dims, spread, reach, shards=(), held_as=jnp.bfloat16):
    factor_of = block_scale(rng, dims, shards, -0.22, 0.18) if shards else 1.0
    drawn = jax.random.normal(rng, dims, jnp.float32) * spread * factor_of
    return jnp.minimum(jnp.maximum(drawn, -reach), reach).astype(held_as)


def setup_inputs(seed: int = 0) -> dict:
    splits = jax.random.split(jax.random.key(seed), 5)
    return {
        "echoes": bell_draw(splits[0], (HALVES, PULSE_H, 2 * FREQS), 1.0, 6.0, ((0, 16), (1, 32)), jnp.float32),
        "pulse_offset": jnp.clip(1.0 * jax.random.uniform(splits[1], (HALVES, PULSE_H), jnp.float32) ** block_scale(splits[1], (HALVES, PULSE_H), ((0, 16), (1, 32)), -0.2, 0.2), 0.0, 1.0),
        "range_gates": plant(jax.random.randint(splits[2], (HALVES, PULSE_H, FREQS), 0, GATES), jax.random.fold_in(splits[2], 1), 0, GATES - 1).astype(jnp.int32),
        "visible": plant((jax.random.randint(splits[3], (HALVES, TILES), 0, 4) < 3).astype(jnp.int32), jax.random.fold_in(splits[3], 1), 0, 1),
    }


grid_cols = 16
two_pi = 2.0 * math.pi


def make_right(sine_wave):
    pixels = jnp.arange(PIX, dtype=jnp.float32)
    phase_grid = sine_wave[:, None] * pixels[None, :]
    real_part = jnp.cos(phase_grid).astype(jnp.bfloat16)
    imag_part = jnp.sin(phase_grid).astype(jnp.bfloat16)
    upper = jnp.concatenate([real_part, imag_part], axis=1)
    lower = jnp.concatenate([-imag_part, real_part], axis=1)
    return jnp.concatenate([upper, lower], axis=0)


def make_base(cosine_wave):
    pixels = jnp.arange(PIX, dtype=jnp.float32)
    base_phase = cosine_wave[None, :] * pixels[:, None]
    return jnp.cos(base_phase), jnp.sin(base_phase)


def make_left(echo_real, echo_imag, cosine_wave, sine_wave, base_cos, base_sin, tile_number, norm_scale):
    column = ((tile_number % grid_cols) * PIX - 8 * PIX).astype(jnp.float32)
    row_start = ((tile_number // grid_cols) * PIX - 4 * PIX).astype(jnp.float32)
    offset_phase = cosine_wave * column + sine_wave * row_start
    offset_cos = jnp.cos(offset_phase)
    offset_sin = jnp.sin(offset_phase)
    turned_real = norm_scale * (echo_real * offset_cos - echo_imag * offset_sin)
    turned_imag = norm_scale * (echo_real * offset_sin + echo_imag * offset_cos)
    real_part = turned_real[None, :] * base_cos - turned_imag[None, :] * base_sin
    imag_part = turned_real[None, :] * base_sin + turned_imag[None, :] * base_cos
    return jnp.concatenate([real_part, imag_part], axis=1).astype(jnp.bfloat16)


def half_image(fields):
    echo_half, offset_half, gates_half, shown_row, half_number = fields
    angle = two_pi * (half_number.astype(jnp.float32) + offset_half) / HALVES
    wave = 0.5 + gates_half.astype(jnp.float32) / GATES
    cosine_wave = (wave * jnp.cos(angle)[:, None]).reshape(-1)
    sine_wave = (wave * jnp.sin(angle)[:, None]).reshape(-1)
    echo_real = echo_half[:, :FREQS].reshape(-1)
    echo_imag = echo_half[:, FREQS:].reshape(-1)
    right_side = make_right(sine_wave)
    base_cos, base_sin = make_base(cosine_wave)
    norm_scale = (2.0 * PULSE_H * FREQS) ** -0.5

    def one_tile(tile_number):
        left_side = make_left(echo_real, echo_imag, cosine_wave, sine_wave, base_cos, base_sin, tile_number, norm_scale)
        return jnp.dot(left_side, right_side, preferred_element_type=jnp.float32)

    result = lax.map(one_tile, jnp.arange(TILES, dtype=jnp.int32))
    return result * shown_row.astype(jnp.float32)[:, None, None]


def reference(echoes, pulse_offset, range_gates, visible):
    halves = lax.map(half_image, (echoes, pulse_offset, range_gates, visible, jnp.arange(HALVES, dtype=jnp.int32)))
    images = halves + jnp.roll(halves, -1, axis=0)
    power_map = images[..., :PIX] ** 2 + images[..., PIX:] ** 2
    peak = jnp.max(power_map, axis=0)
    return images, peak
```

```python
import functools
import math

import jax
import jax.numpy as jnp
from jax import lax
from jax.experimental import pallas as pl
from jax.experimental.pallas import tpu as pltpu
from jax.sharding import PartitionSpec as P

PULSE_H = 32
FREQS = 64
PIX = 128
GATES = 512
LANES = 128
CHUNKS = PULSE_H * FREQS // LANES
TILES_DEV = 8
DEPTH = 256

two_pi = 2.0 * math.pi
F32 = jnp.float32
BF16 = jnp.bfloat16


def sincos(x):
    n = jnp.round(x * F32(2.0 / math.pi))
    r = ((x - n * F32(1.5703125)) - n * F32(4.837512969970703125e-4)) - n * F32(7.54978995489188216e-8)
    r2 = r * r
    s = r + r * r2 * (F32(-1.6666654611e-1) + r2 * (F32(8.3321608736e-3) + r2 * F32(-1.9515295891e-4)))
    c = (1.0 - 0.5 * r2) + r2 * r2 * (F32(4.166664568298827e-2) + r2 * (F32(-1.388731625493765e-3) + r2 * F32(2.443315711809948e-5)))
    q = n.astype(jnp.int32)
    odd = (q & 1) == 1
    cos = jnp.where(odd, s, c)
    sin = jnp.where(odd, c, s)
    cos = jnp.where(((q + 1) & 2) == 2, -cos, cos)
    sin = jnp.where((q & 2) == 2, -sin, sin)
    return cos, sin


def times(a, b):
    return a[0] * b[0] - a[1] * b[1], a[0] * b[1] + a[1] * b[0]


def turned_both(a, b):
    p, q, r, t = a[0] * b[0], a[1] * b[1], a[1] * b[0], a[0] * b[1]
    return (p - q, r + t), (p + q, r - t)


def pack_kernel(sub_ref, echo_ref, offset_ref, gates_ref, shown_ref, out_ref):
    half = (2 * sub_ref[0] + lax.broadcasted_iota(jnp.int32, (2, FREQS), 0)).astype(F32)
    offset = jnp.broadcast_to(offset_ref[...], (2, FREQS))
    angle = two_pi * (half + offset) / 32
    wave = 0.5 + gates_ref[...].astype(F32) / GATES
    cos, sin = sincos(angle)
    waves = jnp.concatenate([wave * cos, wave * sin], axis=1)
    out_ref[...] = jnp.zeros_like(out_ref)
    out_ref[0:1, :] = waves[0:1]
    out_ref[1:2, :] = echo_ref[0:1, :]
    out_ref[2:3, :] = waves[1:2]
    out_ref[3:4, :] = echo_ref[1:2, :]
    out_ref[4:6, 0:TILES_DEV] = shown_ref[...].astype(F32)


def pack(sub, echoes, offset, gates, shown):
    vmem = pl.BlockSpec(memory_space=pltpu.VMEM)
    return pl.pallas_call(
        pack_kernel,
        out_shape=jax.ShapeDtypeStruct((8, LANES), F32),
        in_specs=[pl.BlockSpec(memory_space=pltpu.SMEM)] + [vmem] * 4,
        out_specs=vmem,
    )(sub, echoes, offset, gates, shown)


def spread_kernel(own_ref, next_ref, out_ref):
    tile = jnp.concatenate([own_ref[0:4, :], next_ref[0:4, :]], axis=0)
    out_ref[...] = jnp.broadcast_to(tile[None], out_ref.shape)


def spread(own, following):
    vmem = pl.BlockSpec(memory_space=pltpu.VMEM)
    return pl.pallas_call(
        spread_kernel,
        out_shape=jax.ShapeDtypeStruct((32, 8, LANES), F32),
        in_specs=[vmem] * 2,
        out_specs=vmem,
    )(own, following)


def row(ref, at):
    return jnp.broadcast_to(ref[pl.ds(at, 1), :], (8, LANES))


def image_kernel(place_ref, g_ref, own_ref, next_ref, images_ref, keep_ref, send_ref,
                 left_ref, right_ref, wave_ref, table_ref, prod_ref):
    tile_index = place_ref[0]
    core = place_ref[1]
    x_first = ((tile_index % 2) * 1024 - 1024).astype(F32)
    y_first = ((tile_index // 2) * 128 - 512).astype(F32)
    scale = F32((2.0 * PULSE_H * FREQS) ** -0.5)
    low = lax.broadcasted_iota(jnp.int32, (16, LANES), 1) < FREQS
    sigma = lax.broadcasted_iota(jnp.int32, (8, LANES), 0).astype(F32) - 3.5

    def halved(at):
        m = g_ref[pl.ds(at, 32, stride=8), :]
        t = pltpu.roll(m, FREQS, 1)
        return jnp.where(low, m[:16], t[16:]), jnp.where(low, t[:16], m[16:])

    def build(half):
        ca, sa = halved(2 * half)
        er, ei = halved(2 * half + 1)
        wave_ref[0:16, :] = ca
        wave_ref[16:32, :] = sa

        def put(slot, v):
            table_ref[slot * 32: slot * 32 + 16, :] = v[0]
            table_ref[slot * 32 + 16: slot * 32 + 32, :] = v[1]

        e4 = sincos(ca * 4.0)
        e8 = times(e4, e4)
        v = e4
        for m in range(4):
            put(m, v)
            if m < 3:
                v = times(v, e8)
        e32 = times(v, e4)
        e64 = times(e32, e32)
        v = e32
        for j in range(4):
            put(4 + j, v)
            if j < 3:
                v = times(v, e64)
        e4 = sincos(sa * 4.0)
        e8 = times(e4, e4)
        v = e4
        for m in range(8):
            put(8 + m, v)
            if m < 7:
                v = times(v, e8)
        for block in range(2):
            phase = ca * (x_first + (255.5 + 512.0 * block)) + sa * (y_first + 63.5)
            put(16 + block, times((er * scale, ei * scale), sincos(phase)))

        def chunk(c, carry):
            def entry(slot):
                return row(table_ref, slot * 32 + c), row(table_ref, slot * 32 + 16 + c)

            lanes = pl.ds(pl.multiple_of(c * LANES, LANES), LANES)
            w = sincos(row(wave_ref, c) * sigma)
            for j in range(4):
                a = times(w, entry(4 + j))
                rows = [None] * 8
                for m in range(4):
                    rows[4 + m], rows[3 - m] = turned_both(a, entry(m))
                for b in range(0, 8, 2):
                    at = j * 64 + b * 8
                    for part in range(2):
                        left_ref[part * DEPTH + at: part * DEPTH + at + 16, lanes] = jnp.concatenate(
                            [rows[b][part], rows[b + 1][part]], axis=0).astype(BF16)
            v = sincos(row(wave_ref, 16 + c) * sigma)
            for block in range(2):
                a = times(v, entry(16 + block))
                rows = [None] * 16
                for m in range(8):
                    rows[8 + m], rows[7 - m] = turned_both(a, entry(8 + m))
                for b in range(0, 16, 2):
                    at = block * 256 + b * 8
                    for part in range(2):
                        right_ref[part * 128 + at: part * 128 + at + 16, lanes] = jnp.concatenate(
                            [rows[b][part], rows[b + 1][part]], axis=0).astype(BF16)
            return carry

        lax.fori_loop(0, CHUNKS, chunk, 0)

    def product():
        prod_ref[...] = lax.dot_general(left_ref[...], right_ref[...], (((1,), (1,)), ((), ())),
                                        preferred_element_type=F32)

    def flip(v):
        at = lax.broadcasted_iota(jnp.int32, v.shape, 0)
        v = pltpu.roll(v, 4, 0)
        v = jnp.where((at & 2) == 0, pltpu.roll(v, 6, 0), pltpu.roll(v, 2, 0))
        return jnp.where((at & 1) == 0, pltpu.roll(v, 7, 0), pltpu.roll(v, 1, 0))

    def weight(half, tile):
        ref, at = (own_ref, 4 + half) if half < 2 else (next_ref, 4)
        return ref[at:at + 1, tile:tile + 1]

    def parts(half, block, quarter, r):
        rows = pl.ds(pl.multiple_of(quarter * 128 + r * 8, 8), 8)
        rows2 = pl.ds(pl.multiple_of(DEPTH + quarter * 128 + r * 8, 8), 8)
        pr = prod_ref[rows, block * 256: block * 256 + 128]
        pi = prod_ref[rows, block * 256 + 128: block * 256 + 256]
        qr = prod_ref[rows2, block * 256: block * 256 + 128]
        qi = prod_ref[rows2, block * 256 + 128: block * 256 + 256]
        up = jnp.broadcast_to(weight(half, block * 4 + 2 + quarter), (8, LANES))
        down = jnp.broadcast_to(weight(half, block * 4 + 1 - quarter), (8, LANES))
        return (pr - qi) * up, (pi + qr) * up, flip(pr + qi) * down, flip(pi - qr) * down

    def gather_half(half):
        for block in range(2):
            for quarter in range(2):
                for side in range(2):
                    pass

                def body(r, carry):
                    ur, ui, dr, di = parts(half, block, quarter, r)
                    for tile, at, re, im in (
                        (block * 4 + 2 + quarter, r, ur, ui),
                        (block * 4 + 1 - quarter, 15 - r, dr, di),
                    ):
                        rows = pl.ds(pl.multiple_of(at * 8, 8), 8)
                        if half == 0:
                            images_ref[0, tile, rows, 0:128] = re
                            images_ref[0, tile, rows, 128:256] = im
                        elif half == 1:
                            images_ref[0, tile, rows, 0:128] += re
                            images_ref[0, tile, rows, 128:256] += im
                            images_ref[1, tile, rows, 0:128] = re
                            images_ref[1, tile, rows, 128:256] = im
                        else:
                            re = images_ref[1, tile, rows, 0:128] + re
                            im = images_ref[1, tile, rows, 128:256] + im
                            images_ref[1, tile, rows, 0:128] = re
                            images_ref[1, tile, rows, 128:256] = im
                    return carry

                lax.fori_loop(0, 16, body, 0)

    for half in range(3):
        build(half)
        product()
        gather_half(half)

    for tile in range(TILES_DEV):
        def peaks(z, carry):
            both = []
            for c in range(2):
                rows = pl.ds(pl.multiple_of(z * 16 + c * 8, 8), 8)
                power = [images_ref[s, tile, rows, 0:128] ** 2 + images_ref[s, tile, rows, 128:256] ** 2
                         for s in range(2)]
                both.append(jnp.maximum(power[0], power[1]))
            keep_ref[z, tile] = jnp.where(core == 0, both[0], both[1])
            send_ref[z, tile] = jnp.where(core == 0, both[1], both[0])
            return carry

        lax.fori_loop(0, 8, peaks, 0)


def image(place, gathered, own, following):
    vmem = pl.BlockSpec(memory_space=pltpu.VMEM)
    piece = jax.ShapeDtypeStruct((8, TILES_DEV, 8, LANES), F32)
    return pl.pallas_call(
        image_kernel,
        out_shape=(jax.ShapeDtypeStruct((2, TILES_DEV, PIX, 2 * PIX), F32), piece, piece),
        in_specs=[pl.BlockSpec(memory_space=pltpu.SMEM)] + [vmem] * 3,
        out_specs=(vmem, vmem, vmem),
        scratch_shapes=[
            pltpu.VMEM((2 * DEPTH, PULSE_H * FREQS), BF16),
            pltpu.VMEM((512, PULSE_H * FREQS), BF16),
            pltpu.VMEM((32, LANES), F32),
            pltpu.VMEM((18 * 32, LANES), F32),
            pltpu.VMEM((2 * DEPTH, 512), F32),
        ],
        compiler_params=pltpu.CompilerParams(vmem_limit_bytes=40 * 1024 * 1024),
    )(place, gathered, own, following)


def on_device(echoes, pulse_offset, range_gates, visible):
    sub = lax.axis_index("sub")
    tile = lax.axis_index("tile")
    subs = lax.axis_size("sub")
    own = pack(sub[None].astype(jnp.int32), echoes[:, 0], pulse_offset, range_gates[:, 0], visible)
    following = lax.ppermute(own, "sub", [((i + 1) % subs, i) for i in range(subs)])
    gathered = lax.all_to_all(spread(own, following), "tile", 0, 0, tiled=True)
    place = jnp.stack([tile, sub % 2]).astype(jnp.int32)
    images, keep, send = image(place, gathered.reshape(256, LANES), own, following)
    other = lax.ppermute(send, "sub", [(i, i ^ 1) for i in range(subs)])
    both = jnp.maximum(keep, other)
    groups = [[2 * z + c for z in range(subs // 2)] for c in range(2)]
    pieces = lax.all_to_all(both, "sub", 0, 0, tiled=True, axis_index_groups=groups)
    return images, jnp.max(pieces, axis=0)


def solution(mesh):
    in_specs = (P("sub", "tile", None), P("sub", "tile"), P("sub", "tile", None), P("sub", "tile"))
    out_specs = (P("sub", "tile", None, None), P("tile", "sub", None))
    return jax.shard_map(
        on_device, mesh=mesh, in_specs=in_specs, out_specs=out_specs, check_vma=False
    )
```

```python
import functools
import math

import jax
import jax.numpy as jnp
from jax import lax
from jax.experimental import pallas as pl
from jax.experimental.pallas import tpu as pltpu
from jax.sharding import PartitionSpec as P

PULSE_H = 32
FREQS = 64
PIX = 128
GATES = 512
LANES = 128
CHUNKS = PULSE_H * FREQS // LANES
TILES_DEV = 8
DEPTH = 256

two_pi = 2.0 * math.pi
F32 = jnp.float32
BF16 = jnp.bfloat16


def sincos(x):
    n = jnp.round(x * F32(2.0 / math.pi))
    r = ((x - n * F32(1.5703125)) - n * F32(4.837512969970703125e-4)) - n * F32(7.54978995489188216e-8)
    r2 = r * r
    s = r + r * r2 * (F32(-1.6666654611e-1) + r2 * (F32(8.3321608736e-3) + r2 * F32(-1.9515295891e-4)))
    c = (1.0 - 0.5 * r2) + r2 * r2 * (F32(4.166664568298827e-2) + r2 * (F32(-1.388731625493765e-3) + r2 * F32(2.443315711809948e-5)))
    q = n.astype(jnp.int32)
    odd = (q & 1) == 1
    cos = jnp.where(odd, s, c)
    sin = jnp.where(odd, c, s)
    cos = jnp.where(((q + 1) & 2) == 2, -cos, cos)
    sin = jnp.where((q & 2) == 2, -sin, sin)
    return cos, sin


def times(a, b):
    return a[0] * b[0] - a[1] * b[1], a[0] * b[1] + a[1] * b[0]


def turned_both(a, b):
    p, q, r, t = a[0] * b[0], a[1] * b[1], a[1] * b[0], a[0] * b[1]
    return (p - q, r + t), (p + q, r - t)


def pack_kernel(place_ref, echo_ref, offset_ref, gates_ref, shown_ref, out_ref):
    first = lax.broadcasted_iota(jnp.int32, (2, FREQS), 0)
    half = (2 * place_ref[1] + first).astype(F32)
    offset = jnp.where(first == 0, offset_ref[0:1, 0:1], offset_ref[0:1, 1:2])
    angle = two_pi * (half + offset) / 32
    wave = 0.5 + gates_ref[...].astype(F32) / GATES
    cos, sin = sincos(angle)
    waves = jnp.concatenate([wave * cos, wave * sin], axis=1)
    out_ref[...] = jnp.zeros_like(out_ref)
    out_ref[0:1, :] = waves[0:1]
    out_ref[1:2, :] = echo_ref[0:1, :]
    out_ref[2:3, :] = waves[1:2]
    out_ref[3:4, :] = echo_ref[1:2, :]
    out_ref[4:6, 0:TILES_DEV] = shown_ref[...].astype(F32)


def pack(place, echoes, offset, gates, shown):
    vmem = pl.BlockSpec(memory_space=pltpu.VMEM)
    return pl.pallas_call(
        pack_kernel,
        out_shape=jax.ShapeDtypeStruct((8, LANES), F32),
        in_specs=[pl.BlockSpec(memory_space=pltpu.SMEM)] + [vmem] * 4,
        out_specs=vmem,
        compiler_params=pltpu.CompilerParams(vmem_limit_bytes=4 * 1024 * 1024),
    )(place, echoes, offset, gates, shown)


def spread_kernel(own_ref, next_ref, out_ref):
    shown = jnp.concatenate([own_ref[4:5, 0:FREQS], own_ref[5:6, 0:FREQS]], axis=1)
    tile = jnp.concatenate([own_ref[0:4, :], next_ref[0:2, :], shown, next_ref[4:5, :]], axis=0)
    out_ref[...] = jnp.broadcast_to(tile[None], out_ref.shape)


def spread(own, following):
    vmem = pl.BlockSpec(memory_space=pltpu.VMEM)
    return pl.pallas_call(
        spread_kernel,
        out_shape=jax.ShapeDtypeStruct((32, 8, LANES), F32),
        in_specs=[vmem] * 2,
        out_specs=vmem,
        compiler_params=pltpu.CompilerParams(vmem_limit_bytes=4 * 1024 * 1024),
    )(own, following)


def row(ref, at):
    return jnp.broadcast_to(ref[pl.ds(at, 1), :], (8, LANES))


def image_kernel(place_ref, g_ref, images_ref, keep_ref, send_ref,
                 left_ref, right_ref, wave_ref, table_ref, prod_ref, out_ref, sems):
    tile_index = place_ref[0]
    core = place_ref[1] % 2
    x_first = ((tile_index % 2) * 1024 - 1024).astype(F32)
    y_first = ((tile_index // 2) * 128 - 512).astype(F32)
    scale = F32((2.0 * PULSE_H * FREQS) ** -0.5)
    low = lax.broadcasted_iota(jnp.int32, (16, LANES), 1) < FREQS
    sigma = lax.broadcasted_iota(jnp.int32, (8, LANES), 0).astype(F32) - 3.5
    backwards = 7 - lax.broadcasted_iota(jnp.int32, (8, LANES), 0)

    def halved(at):
        m = g_ref[pl.ds(at, 32, stride=8), :]
        t = pltpu.roll(m, FREQS, 1)
        return jnp.where(low, m[:16], t[16:]), jnp.where(low, t[:16], m[16:])

    def build(half):
        ca, sa = halved(2 * half)
        er, ei = halved(2 * half + 1)
        wave_ref[0:16, :] = ca
        wave_ref[16:32, :] = sa

        def put(slot, v):
            table_ref[slot * 32: slot * 32 + 16, :] = v[0]
            table_ref[slot * 32 + 16: slot * 32 + 32, :] = v[1]

        e4 = sincos(ca * 4.0)
        e8 = times(e4, e4)
        v = e4
        for m in range(4):
            put(m, v)
            if m < 3:
                v = times(v, e8)
        e32 = times(v, e4)
        e64 = times(e32, e32)
        v = e32
        for j in range(4):
            put(4 + j, v)
            if j < 3:
                v = times(v, e64)
        e4 = sincos(sa * 4.0)
        e8 = times(e4, e4)
        v = e4
        for m in range(8):
            put(8 + m, v)
            if m < 7:
                v = times(v, e8)
        for block in range(2):
            phase = ca * (x_first + (255.5 + 512.0 * block)) + sa * (y_first + 63.5)
            put(16 + block, times((er * scale, ei * scale), sincos(phase)))

        def chunk(c, carry):
            def entry(slot):
                return row(table_ref, slot * 32 + c), row(table_ref, slot * 32 + 16 + c)

            w = sincos(row(wave_ref, c) * sigma)
            for j in range(4):
                a = times(w, entry(4 + j))
                rows = [None] * 8
                for m in range(4):
                    rows[4 + m], rows[3 - m] = turned_both(a, entry(m))
                for b in range(0, 8, 2):
                    at = j * 64 + b * 8
                    for part in range(2):
                        left_ref[c, part * DEPTH + at: part * DEPTH + at + 16, :] = jnp.concatenate(
                            [rows[b][part], rows[b + 1][part]], axis=0).astype(BF16)
            v = sincos(row(wave_ref, 16 + c) * sigma)
            for block in range(2):
                a = times(v, entry(16 + block))
                rows = [None] * 16
                for m in range(8):
                    rows[8 + m], rows[7 - m] = turned_both(a, entry(8 + m))
                for b in range(0, 16, 2):
                    at = block * 256 + b * 8
                    for part in range(2):
                        right_ref[c, part * 128 + at: part * 128 + at + 16, :] = jnp.concatenate(
                            [rows[b][part], rows[b + 1][part]], axis=0).astype(BF16)
            return carry

        lax.fori_loop(0, CHUNKS, chunk, 0)

    def product(half):
        left = jnp.concatenate([left_ref[c] for c in range(CHUNKS)], axis=1)
        right = jnp.concatenate([right_ref[c] for c in range(CHUNKS)], axis=1)
        prod_ref[half] = lax.dot_general(left, right, (((1,), (1,)), ((), ())), preferred_element_type=F32)

    def flip(v):
        return jnp.take_along_axis(v, backwards, axis=0)

    def weight(half, tile):
        lane = half * FREQS + tile if half < 2 else tile
        own = g_ref[pl.ds(tile_index * 8 + (6 if half < 2 else 7), 1), :]
        return jnp.broadcast_to(own[:, lane:lane + 1], (8, LANES))

    def out_copy(s, tile):
        return pltpu.make_async_copy(out_ref.at[s, tile], images_ref.at[s, tile], sems.at[s, tile])

    for half in range(3):
        build(half)
        product(half)

    for block in range(2):
        for quarter in range(2):
            upper, lower = block * 4 + 2 + quarter, block * 4 + 1 - quarter
            up = [weight(half, upper) for half in range(3)]
            down = [weight(half, lower) for half in range(3)]

            def finish(z, carry):
                power_up, power_down = [], []
                for c in range(2):
                    r = 2 * z + c
                    near = pl.ds(pl.multiple_of(quarter * 128 + r * 8, 8), 8)
                    far = pl.ds(pl.multiple_of(DEPTH + quarter * 128 + r * 8, 8), 8)
                    above, below = [], []
                    for half in range(3):
                        pr = prod_ref[half, near, block * 256: block * 256 + 128]
                        pi = prod_ref[half, near, block * 256 + 128: block * 256 + 256]
                        qr = prod_ref[half, far, block * 256: block * 256 + 128]
                        qi = prod_ref[half, far, block * 256 + 128: block * 256 + 256]
                        above.append(((pr - qi) * up[half], (pi + qr) * up[half]))
                        below.append(((pr + qi) * down[half], (pi - qr) * down[half]))
                    for sums, tile, at, power, turn in ((above, upper, r, power_up, False),
                                                        (below, lower, 15 - r, power_down, True)):
                        rows = pl.ds(pl.multiple_of(at * 8, 8), 8)
                        most = None
                        for s in range(2):
                            re, im = (sums[s][part] + sums[s + 1][part] for part in range(2))
                            if turn:
                                re, im = flip(re), flip(im)
                            out_ref[s, tile, rows, 0:128] = re
                            out_ref[s, tile, rows, 128:256] = im
                            now = re * re + im * im
                            most = now if most is None else jnp.maximum(most, now)
                        power.append(most)
                keep_ref[z, upper] = jnp.where(core == 0, power_up[0], power_up[1])
                send_ref[z, upper] = jnp.where(core == 0, power_up[1], power_up[0])
                keep_ref[7 - z, lower] = jnp.where(core == 0, power_down[1], power_down[0])
                send_ref[7 - z, lower] = jnp.where(core == 0, power_down[0], power_down[1])
                return carry

            lax.fori_loop(0, 8, finish, 0)
            for s in range(2):
                out_copy(s, upper).start()
                out_copy(s, lower).start()
    for s in range(2):
        for tile in range(TILES_DEV):
            out_copy(s, tile).wait()


def image(place, gathered):
    vmem = pl.BlockSpec(memory_space=pltpu.VMEM)
    piece = jax.ShapeDtypeStruct((8, TILES_DEV, 8, LANES), F32)
    return pl.pallas_call(
        image_kernel,
        out_shape=(jax.ShapeDtypeStruct((2, TILES_DEV, PIX, 2 * PIX), F32), piece, piece),
        in_specs=[pl.BlockSpec(memory_space=pltpu.SMEM), vmem],
        out_specs=(pl.BlockSpec(memory_space=pl.ANY), vmem, vmem),
        scratch_shapes=[
            pltpu.VMEM((CHUNKS, 2 * DEPTH, LANES), BF16),
            pltpu.VMEM((CHUNKS, 512, LANES), BF16),
            pltpu.VMEM((32, LANES), F32),
            pltpu.VMEM((18 * 32, LANES), F32),
            pltpu.VMEM((3, 2 * DEPTH, 512), F32),
            pltpu.VMEM((2, TILES_DEV, PIX, 2 * PIX), F32),
            pltpu.SemaphoreType.DMA((2, TILES_DEV)),
        ],
        compiler_params=pltpu.CompilerParams(vmem_limit_bytes=40 * 1024 * 1024),
    )(place, gathered)


def on_device(echoes, pulse_offset, range_gates, visible):
    sub = lax.axis_index("sub")
    tile = lax.axis_index("tile")
    subs = lax.axis_size("sub")
    place = jnp.stack([tile, sub]).astype(jnp.int32)
    own = pack(place, echoes[:, 0], pulse_offset.reshape(1, 2), range_gates[:, 0], visible)
    following = lax.ppermute(own, "sub", [((i + 1) % subs, i) for i in range(subs)])
    gathered = lax.all_to_all(spread(own, following), "tile", 0, 0, tiled=True)
    images, keep, send = image(place, gathered.reshape(256, LANES))
    other = lax.ppermute(send, "sub", [(i, i ^ 1) for i in range(subs)])
    both = jnp.maximum(keep, other)
    groups = [[2 * z + c for z in range(subs // 2)] for c in range(2)]
    pieces = lax.all_to_all(both, "sub", 0, 0, tiled=True, axis_index_groups=groups)
    return images, jnp.max(pieces, axis=0)


def solution(mesh):
    in_specs = (P("sub", "tile", None), P("sub", "tile"), P("sub", "tile", None), P("sub", "tile"))
    out_specs = (P("sub", "tile", None, None), P("tile", "sub", None))
    return jax.shard_map(
        on_device, mesh=mesh, in_specs=in_specs, out_specs=out_specs, check_vma=False
    )
```

```python
import functools
import math

import jax
import jax.numpy as jnp
from jax import lax
from jax.experimental import pallas as pl
from jax.experimental.pallas import tpu as pltpu
from jax.sharding import PartitionSpec as P

PULSE_H = 32
FREQS = 64
PIX = 128
GATES = 512
LANES = 128
CHUNKS = PULSE_H * FREQS // LANES
TILES_DEV = 8
DEPTH = 256

two_pi = 2.0 * math.pi
F32 = jnp.float32
BF16 = jnp.bfloat16


def sincos(x):
    n = jnp.round(x * F32(2.0 / math.pi))
    r = ((x - n * F32(1.5703125)) - n * F32(4.837512969970703125e-4)) - n * F32(7.54978995489188216e-8)
    r2 = r * r
    s = r + r * r2 * (F32(-1.6666654611e-1) + r2 * (F32(8.3321608736e-3) + r2 * F32(-1.9515295891e-4)))
    c = (1.0 - 0.5 * r2) + r2 * r2 * (F32(4.166664568298827e-2) + r2 * (F32(-1.388731625493765e-3) + r2 * F32(2.443315711809948e-5)))
    q = n.astype(jnp.int32)
    odd = (q & 1) == 1
    cos = jnp.where(odd, s, c)
    sin = jnp.where(odd, c, s)
    cos = jnp.where(((q + 1) & 2) == 2, -cos, cos)
    sin = jnp.where((q & 2) == 2, -sin, sin)
    return cos, sin


def times(a, b):
    return a[0] * b[0] - a[1] * b[1], a[0] * b[1] + a[1] * b[0]


def turned_both(a, b):
    p, q, r, t = a[0] * b[0], a[1] * b[1], a[1] * b[0], a[0] * b[1]
    return (p - q, r + t), (p + q, r - t)


def pack_kernel(place_ref, echo_ref, offset_ref, gates_ref, shown_ref, out_ref):
    first = lax.broadcasted_iota(jnp.int32, (2, FREQS), 0)
    half = (2 * place_ref[1] + first).astype(F32)
    offset = jnp.where(first == 0, offset_ref[0:1, 0:1], offset_ref[0:1, 1:2])
    angle = two_pi * (half + offset) / 32
    wave = 0.5 + gates_ref[...].astype(F32) / GATES
    cos, sin = sincos(angle)
    waves = jnp.concatenate([wave * cos, wave * sin], axis=1)
    out_ref[...] = jnp.zeros_like(out_ref)
    out_ref[0:1, :] = waves[0:1]
    out_ref[1:2, :] = echo_ref[0:1, :]
    out_ref[2:3, :] = waves[1:2]
    out_ref[3:4, :] = echo_ref[1:2, :]
    out_ref[4:6, 0:TILES_DEV] = shown_ref[...].astype(F32)


def pack(place, echoes, offset, gates, shown):
    vmem = pl.BlockSpec(memory_space=pltpu.VMEM)
    return pl.pallas_call(
        pack_kernel,
        out_shape=jax.ShapeDtypeStruct((8, LANES), F32),
        in_specs=[pl.BlockSpec(memory_space=pltpu.SMEM)] + [vmem] * 4,
        out_specs=vmem,
    )(place, echoes, offset, gates, shown)


def spread_kernel(own_ref, next_ref, out_ref):
    shown = jnp.concatenate([own_ref[4:5, 0:FREQS], own_ref[5:6, 0:FREQS]], axis=1)
    tile = jnp.concatenate([own_ref[0:4, :], next_ref[0:2, :], shown, next_ref[4:5, :]], axis=0)
    out_ref[...] = jnp.broadcast_to(tile[None], out_ref.shape)


def spread(own, following):
    vmem = pl.BlockSpec(memory_space=pltpu.VMEM)
    return pl.pallas_call(
        spread_kernel,
        out_shape=jax.ShapeDtypeStruct((32, 8, LANES), F32),
        in_specs=[vmem] * 2,
        out_specs=vmem,
        compiler_params=pltpu.CompilerParams(vmem_limit_bytes=4 * 1024 * 1024),
    )(own, following)


def row(ref, at):
    return jnp.broadcast_to(ref[pl.ds(at, 1), :], (8, LANES))


def image_kernel(place_ref, g_ref, images_ref, keep_ref, send_ref,
                 left_a, left_b, right_a, right_b, wave_ref, table_ref, prod_ref, out_ref, power_ref, sems):
    tile_index = place_ref[0]
    core = place_ref[1] % 2
    x_first = ((tile_index % 2) * 1024 - 1024).astype(F32)
    y_first = ((tile_index // 2) * 128 - 512).astype(F32)
    scale = F32((2.0 * PULSE_H * FREQS) ** -0.5)
    low = lax.broadcasted_iota(jnp.int32, (16, LANES), 1) < FREQS
    sigma = lax.broadcasted_iota(jnp.int32, (8, LANES), 0).astype(F32) - 3.5
    backwards = 7 - lax.broadcasted_iota(jnp.int32, (8, LANES), 0)

    def halved(at):
        m = g_ref[pl.ds(at, 32, stride=8), :]
        t = pltpu.roll(m, FREQS, 1)
        return jnp.where(low, m[:16], t[16:]), jnp.where(low, t[:16], m[16:])

    def tables(half):
        ca, sa = halved(2 * half)
        er, ei = halved(2 * half + 1)
        wave_ref[0:16, :] = ca
        wave_ref[16:32, :] = sa

        def put(slot, v):
            table_ref[slot * 32: slot * 32 + 16, :] = v[0]
            table_ref[slot * 32 + 16: slot * 32 + 32, :] = v[1]

        e4 = sincos(ca * 4.0)
        e8 = times(e4, e4)
        v = e4
        for m in range(4):
            put(m, v)
            if m < 3:
                v = times(v, e8)
        e32 = times(v, e4)
        e64 = times(e32, e32)
        v = e32
        for j in range(4):
            put(4 + j, v)
            if j < 3:
                v = times(v, e64)
        e4 = sincos(sa * 4.0)
        e8 = times(e4, e4)
        v = e4
        for m in range(8):
            put(8 + m, v)
            if m < 7:
                v = times(v, e8)
        for block in range(2):
            phase = ca * (x_first + (255.5 + 512.0 * block)) + sa * (y_first + 63.5)
            put(16 + block, times((er * scale, ei * scale), sincos(phase)))

    def chunk(c, left_ref, right_ref):
        def entry(slot):
            return row(table_ref, slot * 32 + c), row(table_ref, slot * 32 + 16 + c)

        w = sincos(row(wave_ref, c) * sigma)
        for j in range(4):
            a = times(w, entry(4 + j))
            for m in (0, 2):
                near, far = turned_both(a, entry(m)), turned_both(a, entry(m + 1))
                for b, rows in ((4 + m, (near[0], far[0])), (2 - m, (far[1], near[1]))):
                    at = j * 64 + b * 8
                    for part in range(2):
                        left_ref[c, part * DEPTH + at: part * DEPTH + at + 16, :] = jnp.concatenate(
                            [rows[0][part], rows[1][part]], axis=0).astype(BF16)
        v = sincos(row(wave_ref, 16 + c) * sigma)
        for block in range(2):
            a = times(v, entry(16 + block))
            for m in (0, 2, 4, 6):
                near, far = turned_both(a, entry(8 + m)), turned_both(a, entry(9 + m))
                for b, rows in ((8 + m, (near[0], far[0])), (6 - m, (far[1], near[1]))):
                    at = block * 256 + b * 8
                    for part in range(2):
                        right_ref[c, part * 128 + at: part * 128 + at + 16, :] = jnp.concatenate(
                            [rows[0][part], rows[1][part]], axis=0).astype(BF16)

    def product(left_ref, right_ref, rows, columns):
        left = jnp.concatenate([left_ref[c, rows, :] for c in range(CHUNKS)], axis=1)
        right = jnp.concatenate([right_ref[c, columns, :] for c in range(CHUNKS)], axis=1)
        return lax.dot_general(left, right, (((1,), (1,)), ((), ())), preferred_element_type=F32)

    def stage(done, made):
        sides = ((left_a, right_a), (left_b, right_b))
        tables(made)
        if done is None:
            lax.fori_loop(0, CHUNKS, lambda c, carry: (chunk(c, *sides[made % 2]), carry)[1], 0)
        else:
            def step(i, carry):
                rows, columns = pl.ds(0, 512), pl.ds(pl.multiple_of(i * 256, 256), 256)
                prod_ref[done, rows, columns] = product(*sides[done % 2], rows, columns)
                for c in range(8):
                    chunk(i * 8 + c, *sides[made % 2])
                return carry

            lax.fori_loop(0, 2, step, 0)

    def flip(v):
        return jnp.take_along_axis(v, backwards, axis=0)

    def weight(half, tile):
        lane = half * FREQS + tile if half < 2 else tile
        own = g_ref[pl.ds(tile_index * 8 + (6 if half < 2 else 7), 1), :]
        return jnp.broadcast_to(own[:, lane:lane + 1], (8, LANES))

    def out_copy(s, tile):
        return pltpu.make_async_copy(out_ref.at[s, tile], images_ref.at[s, tile], sems.at[s, tile])

    def finish(s, block):
        for quarter in range(2):
            upper, lower = block * 4 + 2 + quarter, block * 4 + 1 - quarter
            up = [weight(half, upper) for half in (s, s + 1)]
            down = [weight(half, lower) for half in (s, s + 1)]
            for z in range(8):
                power_up, power_down = [], []
                for r in (2 * z, 2 * z + 1):
                    near = slice(quarter * 128 + r * 8, quarter * 128 + r * 8 + 8)
                    far = slice(DEPTH + near.start, DEPTH + near.stop)
                    above, below = [], []
                    for i in range(2):
                        pr = prod_ref[s + i, near, block * 256: block * 256 + 128]
                        pi = prod_ref[s + i, near, block * 256 + 128: block * 256 + 256]
                        qr = prod_ref[s + i, far, block * 256: block * 256 + 128]
                        qi = prod_ref[s + i, far, block * 256 + 128: block * 256 + 256]
                        above.append(((pr - qi) * up[i], (pi + qr) * up[i]))
                        below.append(((pr + qi) * down[i], (pi - qr) * down[i]))
                    for sums, tile, at, power, turn in ((above, upper, r, power_up, False),
                                                        (below, lower, 15 - r, power_down, True)):
                        rows = slice(at * 8, at * 8 + 8)
                        re, im = (sums[0][part] + sums[1][part] for part in range(2))
                        if turn:
                            re, im = flip(re), flip(im)
                        out_ref[s, tile, rows, 0:128] = re
                        out_ref[s, tile, rows, 128:256] = im
                        now = re * re + im * im
                        if s == 0:
                            power_ref[tile, rows, :] = now
                        else:
                            power.append(jnp.maximum(power_ref[tile, rows, :], now))
                if s == 1:
                    keep_ref[z, upper] = jnp.where(core == 0, power_up[0], power_up[1])
                    send_ref[z, upper] = jnp.where(core == 0, power_up[1], power_up[0])
                    keep_ref[7 - z, lower] = jnp.where(core == 0, power_down[1], power_down[0])
                    send_ref[7 - z, lower] = jnp.where(core == 0, power_down[0], power_down[1])

    def leave(s, block):
        for tile in range(block * 4, block * 4 + 4):
            out_copy(s, tile).start()

    def last_product(block):
        columns = slice(block * 256, block * 256 + 256)
        prod_ref[2, :, columns] = product(left_a, right_a, slice(0, 2 * DEPTH), columns)

    stage(None, 0)
    stage(0, 1)
    stage(1, 2)
    last_product(0)
    finish(0, 0)
    finish(0, 1)
    leave(0, 0)
    leave(0, 1)
    last_product(1)
    finish(1, 0)
    leave(1, 0)
    finish(1, 1)
    leave(1, 1)
    for s in range(2):
        for tile in range(TILES_DEV):
            out_copy(s, tile).wait()


def image(place, gathered):
    vmem = pl.BlockSpec(memory_space=pltpu.VMEM)
    piece = jax.ShapeDtypeStruct((8, TILES_DEV, 8, LANES), F32)
    return pl.pallas_call(
        image_kernel,
        out_shape=(jax.ShapeDtypeStruct((2, TILES_DEV, PIX, 2 * PIX), F32), piece, piece),
        in_specs=[pl.BlockSpec(memory_space=pltpu.SMEM), vmem],
        out_specs=(pl.BlockSpec(memory_space=pl.ANY), vmem, vmem),
        scratch_shapes=[
            pltpu.VMEM((CHUNKS, 2 * DEPTH, LANES), BF16),
            pltpu.VMEM((CHUNKS, 2 * DEPTH, LANES), BF16),
            pltpu.VMEM((CHUNKS, 512, LANES), BF16),
            pltpu.VMEM((CHUNKS, 512, LANES), BF16),
            pltpu.VMEM((32, LANES), F32),
            pltpu.VMEM((18 * 32, LANES), F32),
            pltpu.VMEM((3, 2 * DEPTH, 512), F32),
            pltpu.VMEM((2, TILES_DEV, PIX, 2 * PIX), F32),
            pltpu.VMEM((TILES_DEV, PIX, PIX), F32),
            pltpu.SemaphoreType.DMA((2, TILES_DEV)),
        ],
        compiler_params=pltpu.CompilerParams(vmem_limit_bytes=40 * 1024 * 1024),
    )(place, gathered)


def on_device(echoes, pulse_offset, range_gates, visible):
    sub = lax.axis_index("sub")
    tile = lax.axis_index("tile")
    subs = lax.axis_size("sub")
    place = jnp.stack([tile, sub]).astype(jnp.int32)
    own = pack(place, echoes[:, 0], pulse_offset.reshape(1, 2), range_gates[:, 0], visible)
    following = lax.ppermute(own, "sub", [((i + 1) % subs, i) for i in range(subs)])
    gathered = lax.all_to_all(spread(own, following), "tile", 0, 0, tiled=True)
    images, keep, send = image(place, gathered.reshape(256, LANES))
    other = lax.ppermute(send, "sub", [(i, i ^ 1) for i in range(subs)])
    both = jnp.maximum(keep, other)
    groups = [[2 * z + c for z in range(subs // 2)] for c in range(2)]
    pieces = lax.all_to_all(both, "sub", 0, 0, tiled=True, axis_index_groups=groups)
    return images, jnp.max(pieces, axis=0)


def solution(mesh):
    in_specs = (P("sub", "tile", None), P("sub", "tile"), P("sub", "tile", None), P("sub", "tile"))
    out_specs = (P("sub", "tile", None, None), P("tile", "sub", None))
    return jax.shard_map(
        on_device, mesh=mesh, in_specs=in_specs, out_specs=out_specs, check_vma=False
    )
```

```python
import functools
import math

import jax
import jax.numpy as jnp
from jax import lax
from jax.experimental import pallas as pl
from jax.experimental.pallas import tpu as pltpu
from jax.sharding import PartitionSpec as P

PULSE_H = 32
FREQS = 64
PIX = 128
GATES = 512
LANES = 128
CHUNKS = PULSE_H * FREQS // LANES
TILES_DEV = 8
DEPTH = 256

two_pi = 2.0 * math.pi
F32 = jnp.float32
BF16 = jnp.bfloat16


def sincos(x):
    n = jnp.round(x * F32(2.0 / math.pi))
    r = ((x - n * F32(1.5703125)) - n * F32(4.837512969970703125e-4)) - n * F32(7.54978995489188216e-8)
    r2 = r * r
    s = r + r * r2 * (F32(-1.6666654611e-1) + r2 * (F32(8.3321608736e-3) + r2 * F32(-1.9515295891e-4)))
    c = (1.0 - 0.5 * r2) + r2 * r2 * (F32(4.166664568298827e-2) + r2 * (F32(-1.388731625493765e-3) + r2 * F32(2.443315711809948e-5)))
    q = n.astype(jnp.int32)
    odd = (q & 1) == 1
    cos = jnp.where(odd, s, c)
    sin = jnp.where(odd, c, s)
    cos = jnp.where(((q + 1) & 2) == 2, -cos, cos)
    sin = jnp.where((q & 2) == 2, -sin, sin)
    return cos, sin


def times(a, b):
    return a[0] * b[0] - a[1] * b[1], a[0] * b[1] + a[1] * b[0]


def turned_both(a, b):
    p, q, r, t = a[0] * b[0], a[1] * b[1], a[1] * b[0], a[0] * b[1]
    return (p - q, r + t), (p + q, r - t)


def pack_kernel(sub_ref, echo_hbm, offset_hbm, gates_hbm, shown_hbm, out_ref,
                echo_ref, offset_ref, gates_ref, shown_ref, sems):
    copies = [pltpu.make_async_copy(src, dst, sems.at[i]) for i, (src, dst) in enumerate((
        (echo_hbm, echo_ref), (offset_hbm, offset_ref), (gates_hbm, gates_ref), (shown_hbm, shown_ref)))]
    for copy in copies:
        copy.start()
    for copy in copies:
        copy.wait()
    first = lax.broadcasted_iota(jnp.int32, (2, FREQS), 0)
    half = (2 * sub_ref[0] + first).astype(F32)
    offset = jnp.where(first == 0, offset_ref[0:1, 0:1], offset_ref[0:1, 1:2])
    angle = two_pi * (half + offset) / 32
    wave = 0.5 + gates_ref[...].astype(F32) / GATES
    cos, sin = sincos(angle)
    waves = jnp.concatenate([wave * cos, wave * sin], axis=1)
    at = lax.broadcasted_iota(jnp.int32, (8, LANES), 0)
    tile = jnp.zeros((8, LANES), F32)
    for i in range(2):
        tile = jnp.where(at == 2 * i, waves[i:i + 1], tile)
        tile = jnp.where(at == 2 * i + 1, echo_ref[i:i + 1, :], tile)
    out_ref[...] = jnp.broadcast_to(tile[None], out_ref.shape)
    shown = shown_ref[...].astype(F32)
    out_ref[:, 4:6, 0:TILES_DEV] = jnp.broadcast_to(shown[None], (32, 2, TILES_DEV))


def pack(sub, echoes, offset, gates, shown):
    vmem = pl.BlockSpec(memory_space=pltpu.VMEM)
    return pl.pallas_call(
        pack_kernel,
        out_shape=jax.ShapeDtypeStruct((32, 8, LANES), F32),
        in_specs=[pl.BlockSpec(memory_space=pltpu.SMEM)] + [pl.BlockSpec(memory_space=pltpu.HBM)] * 4,
        out_specs=vmem,
        scratch_shapes=[
            pltpu.VMEM((2, LANES), F32),
            pltpu.VMEM((1, 2), F32),
            pltpu.VMEM((2, FREQS), jnp.int32),
            pltpu.VMEM((2, TILES_DEV), jnp.int32),
            pltpu.SemaphoreType.DMA((4,)),
        ],
    )(sub, echoes, offset, gates, shown)


def row(ref, at):
    return jnp.broadcast_to(ref[pl.ds(at, 1), :], (8, LANES))


def image_kernel(tile_ref, sub_ref, g_ref, next_ref, images_ref, keep_ref, send_ref,
                 left_a, left_b, right_a, right_b, wave_ref, table_ref, prod_ref, out_ref, power_ref, sems):
    tile_index = tile_ref[0]
    core = sub_ref[0] % 2
    x_first = ((tile_index % 2) * 1024 - 1024).astype(F32)
    y_first = ((tile_index // 2) * 128 - 512).astype(F32)
    scale = F32((2.0 * PULSE_H * FREQS) ** -0.5)
    low = lax.broadcasted_iota(jnp.int32, (16, LANES), 1) < FREQS
    sigma = lax.broadcasted_iota(jnp.int32, (8, LANES), 0).astype(F32) - 3.5
    backwards = 7 - lax.broadcasted_iota(jnp.int32, (8, LANES), 0)

    def halved(ref, at):
        m = ref[pl.ds(at, 32, stride=8), :]
        t = pltpu.roll(m, FREQS, 1)
        return jnp.where(low, m[:16], t[16:]), jnp.where(low, t[:16], m[16:])

    def tables(half):
        ref, at = (g_ref, 2 * half) if half < 2 else (next_ref, 0)
        ca, sa = halved(ref, at)
        er, ei = halved(ref, at + 1)
        wave_ref[0:16, :] = ca
        wave_ref[16:32, :] = sa

        def put(slot, v):
            table_ref[slot * 32: slot * 32 + 16, :] = v[0]
            table_ref[slot * 32 + 16: slot * 32 + 32, :] = v[1]

        e4 = sincos(ca * 4.0)
        e8 = times(e4, e4)
        v = e4
        for m in range(4):
            put(m, v)
            if m < 3:
                v = times(v, e8)
        e32 = times(v, e4)
        e64 = times(e32, e32)
        v = e32
        for j in range(4):
            put(4 + j, v)
            if j < 3:
                v = times(v, e64)
        e4 = sincos(sa * 4.0)
        e8 = times(e4, e4)
        v = e4
        for m in range(8):
            put(8 + m, v)
            if m < 7:
                v = times(v, e8)
        for block in range(2):
            phase = ca * (x_first + (255.5 + 512.0 * block)) + sa * (y_first + 63.5)
            put(16 + block, times((er * scale, ei * scale), sincos(phase)))

    def chunk(c, left_ref, right_ref):
        def entry(slot):
            return row(table_ref, slot * 32 + c), row(table_ref, slot * 32 + 16 + c)

        w = sincos(row(wave_ref, c) * sigma)
        for j in range(4):
            a = times(w, entry(4 + j))
            for m in (0, 2):
                near, far = turned_both(a, entry(m)), turned_both(a, entry(m + 1))
                for b, rows in ((4 + m, (near[0], far[0])), (2 - m, (far[1], near[1]))):
                    at = j * 64 + b * 8
                    for part in range(2):
                        left_ref[c, part * DEPTH + at: part * DEPTH + at + 16, :] = jnp.concatenate(
                            [rows[0][part], rows[1][part]], axis=0).astype(BF16)
        v = sincos(row(wave_ref, 16 + c) * sigma)
        for block in range(2):
            a = times(v, entry(16 + block))
            for m in (0, 2, 4, 6):
                near, far = turned_both(a, entry(8 + m)), turned_both(a, entry(9 + m))
                for b, rows in ((8 + m, (near[0], far[0])), (6 - m, (far[1], near[1]))):
                    at = block * 256 + b * 8
                    for part in range(2):
                        right_ref[c, part * 128 + at: part * 128 + at + 16, :] = jnp.concatenate(
                            [rows[0][part], rows[1][part]], axis=0).astype(BF16)

    def product(left_ref, right_ref, rows, columns):
        left = jnp.concatenate([left_ref[c, rows, :] for c in range(CHUNKS)], axis=1)
        right = jnp.concatenate([right_ref[c, columns, :] for c in range(CHUNKS)], axis=1)
        return lax.dot_general(left, right, (((1,), (1,)), ((), ())), preferred_element_type=F32)

    def stage(done, made):
        sides = ((left_a, right_a), (left_b, right_b))
        tables(made)
        if done is None:
            lax.fori_loop(0, CHUNKS, lambda c, carry: (chunk(c, *sides[made % 2]), carry)[1], 0)
        else:
            def step(i, carry):
                rows, columns = pl.ds(0, 512), pl.ds(pl.multiple_of(i * 256, 256), 256)
                prod_ref[done, rows, columns] = product(*sides[done % 2], rows, columns)
                for c in range(8):
                    chunk(i * 8 + c, *sides[made % 2])
                return carry

            lax.fori_loop(0, 2, step, 0)

    def flip(v):
        return jnp.take_along_axis(v, backwards, axis=0)

    def weight(half, tile):
        ref, at = (g_ref, 4 + half) if half < 2 else (next_ref, 4)
        own = ref[pl.ds(tile_index * 8 + at, 1), :]
        return jnp.broadcast_to(own[:, tile:tile + 1], (8, LANES))

    def out_copy(s, tile):
        return pltpu.make_async_copy(out_ref.at[s, tile], images_ref.at[s, tile], sems.at[s, tile])

    def finish(s, block):
        for quarter in range(2):
            upper, lower = block * 4 + 2 + quarter, block * 4 + 1 - quarter
            up = [weight(half, upper) for half in (s, s + 1)]
            down = [weight(half, lower) for half in (s, s + 1)]
            for z in range(8):
                power_up, power_down = [], []
                for r in (2 * z, 2 * z + 1):
                    near = slice(quarter * 128 + r * 8, quarter * 128 + r * 8 + 8)
                    far = slice(DEPTH + near.start, DEPTH + near.stop)
                    above, below = [], []
                    for i in range(2):
                        pr = prod_ref[s + i, near, block * 256: block * 256 + 128]
                        pi = prod_ref[s + i, near, block * 256 + 128: block * 256 + 256]
                        qr = prod_ref[s + i, far, block * 256: block * 256 + 128]
                        qi = prod_ref[s + i, far, block * 256 + 128: block * 256 + 256]
                        above.append(((pr - qi) * up[i], (pi + qr) * up[i]))
                        below.append(((pr + qi) * down[i], (pi - qr) * down[i]))
                    for sums, tile, at, power, turn in ((above, upper, r, power_up, False),
                                                        (below, lower, 15 - r, power_down, True)):
                        rows = slice(at * 8, at * 8 + 8)
                        re, im = (sums[0][part] + sums[1][part] for part in range(2))
                        if turn:
                            re, im = flip(re), flip(im)
                        out_ref[s, tile, rows, 0:128] = re
                        out_ref[s, tile, rows, 128:256] = im
                        now = re * re + im * im
                        if s == 0:
                            power_ref[tile, rows, :] = now
                        else:
                            power.append(jnp.maximum(power_ref[tile, rows, :], now))
                if s == 1:
                    keep_ref[z, upper] = jnp.where(core == 0, power_up[0], power_up[1])
                    send_ref[z, upper] = jnp.where(core == 0, power_up[1], power_up[0])
                    keep_ref[7 - z, lower] = jnp.where(core == 0, power_down[1], power_down[0])
                    send_ref[7 - z, lower] = jnp.where(core == 0, power_down[0], power_down[1])

    def leave(s, block):
        for tile in range(block * 4, block * 4 + 4):
            out_copy(s, tile).start()

    def last_product(block):
        columns = slice(block * 256, block * 256 + 256)
        prod_ref[2, :, columns] = product(left_a, right_a, slice(0, 2 * DEPTH), columns)

    stage(None, 0)
    stage(0, 1)
    stage(1, 2)
    last_product(0)
    finish(0, 0)
    finish(0, 1)
    leave(0, 0)
    leave(0, 1)
    last_product(1)
    finish(1, 0)
    leave(1, 0)
    finish(1, 1)
    leave(1, 1)
    for s in range(2):
        for tile in range(TILES_DEV):
            out_copy(s, tile).wait()


def image(tile, sub, gathered, following):
    vmem = pl.BlockSpec(memory_space=pltpu.VMEM)
    piece = jax.ShapeDtypeStruct((8, TILES_DEV, 8, LANES), F32)
    return pl.pallas_call(
        image_kernel,
        out_shape=(jax.ShapeDtypeStruct((2, TILES_DEV, PIX, 2 * PIX), F32), piece, piece),
        in_specs=[pl.BlockSpec(memory_space=pltpu.SMEM)] * 2 + [vmem] * 2,
        out_specs=(pl.BlockSpec(memory_space=pl.ANY), vmem, vmem),
        scratch_shapes=[
            pltpu.VMEM((CHUNKS, 2 * DEPTH, LANES), BF16),
            pltpu.VMEM((CHUNKS, 2 * DEPTH, LANES), BF16),
            pltpu.VMEM((CHUNKS, 512, LANES), BF16),
            pltpu.VMEM((CHUNKS, 512, LANES), BF16),
            pltpu.VMEM((32, LANES), F32),
            pltpu.VMEM((18 * 32, LANES), F32),
            pltpu.VMEM((3, 2 * DEPTH, 512), F32),
            pltpu.VMEM((2, TILES_DEV, PIX, 2 * PIX), F32),
            pltpu.VMEM((TILES_DEV, PIX, PIX), F32),
            pltpu.SemaphoreType.DMA((2, TILES_DEV)),
        ],
        compiler_params=pltpu.CompilerParams(vmem_limit_bytes=40 * 1024 * 1024),
    )(tile, sub, gathered, following)


def on_device(echoes, pulse_offset, range_gates, visible):
    sub = lax.axis_index("sub").astype(jnp.int32)[None]
    tile = lax.axis_index("tile").astype(jnp.int32)[None]
    subs = lax.axis_size("sub")
    own = pack(sub, echoes[:, 0], pulse_offset.reshape(1, 2), range_gates[:, 0], visible)
    gathered = lax.all_to_all(own, "tile", 0, 0, tiled=True).reshape(256, LANES)
    following = lax.ppermute(gathered, "sub", [((i + 1) % subs, i) for i in range(subs)])
    images, keep, send = image(tile, sub, gathered, following)
    other = lax.ppermute(send, "sub", [(i, i ^ 1) for i in range(subs)])
    both = jnp.maximum(keep, other)
    groups = [[2 * z + c for z in range(subs // 2)] for c in range(2)]
    pieces = lax.all_to_all(both, "sub", 0, 0, tiled=True, axis_index_groups=groups)
    return images, jnp.max(pieces, axis=0)


def solution(mesh):
    in_specs = (P("sub", "tile", None), P("sub", "tile"), P("sub", "tile", None), P("sub", "tile"))
    out_specs = (P("sub", "tile", None, None), P("tile", "sub", None))
    return jax.shard_map(
        on_device, mesh=mesh, in_specs=in_specs, out_specs=out_specs, check_vma=False
    )
```

```python
import functools
import math

import jax
import jax.numpy as jnp
from jax import lax
from jax.experimental import pallas as pl
from jax.experimental.pallas import tpu as pltpu
from jax.sharding import PartitionSpec as P

PULSE_H = 32
FREQS = 64
PIX = 128
GATES = 512
LANES = 128
CHUNKS = PULSE_H * FREQS // LANES
TILES_DEV = 8
DEPTH = 256

two_pi = 2.0 * math.pi
F32 = jnp.float32
BF16 = jnp.bfloat16


def sincos(x):
    n = jnp.round(x * F32(2.0 / math.pi))
    r = ((x - n * F32(1.5703125)) - n * F32(4.837512969970703125e-4)) - n * F32(7.54978995489188216e-8)
    r2 = r * r
    s = r + r * r2 * (F32(-1.6666654611e-1) + r2 * (F32(8.3321608736e-3) + r2 * F32(-1.9515295891e-4)))
    c = (1.0 - 0.5 * r2) + r2 * r2 * (F32(4.166664568298827e-2) + r2 * (F32(-1.388731625493765e-3) + r2 * F32(2.443315711809948e-5)))
    q = n.astype(jnp.int32)
    odd = (q & 1) == 1
    cos = jnp.where(odd, s, c)
    sin = jnp.where(odd, c, s)
    cos = jnp.where(((q + 1) & 2) == 2, -cos, cos)
    sin = jnp.where((q & 2) == 2, -sin, sin)
    return cos, sin


def times(a, b):
    return a[0] * b[0] - a[1] * b[1], a[0] * b[1] + a[1] * b[0]


def turned_both(a, b):
    p, q, r, t = a[0] * b[0], a[1] * b[1], a[1] * b[0], a[0] * b[1]
    return (p - q, r + t), (p + q, r - t)


def pack_kernel(sub_ref, echo_hbm, offset_hbm, gates_hbm, shown_hbm, out_ref,
                echo_ref, offset_ref, gates_ref, shown_ref, sems):
    copies = [pltpu.make_async_copy(src, dst, sems.at[i]) for i, (src, dst) in enumerate((
        (echo_hbm, echo_ref), (offset_hbm, offset_ref), (gates_hbm, gates_ref), (shown_hbm, shown_ref)))]
    for copy in copies:
        copy.start()
    for copy in copies:
        copy.wait()
    first = lax.broadcasted_iota(jnp.int32, (2, FREQS), 0)
    half = (2 * sub_ref[0] + first).astype(F32)
    offset = jnp.where(first == 0, offset_ref[0:1, 0:1], offset_ref[0:1, 1:2])
    angle = two_pi * (half + offset) / 32
    wave = 0.5 + gates_ref[...].astype(F32) / GATES
    cos, sin = sincos(angle)
    waves = jnp.concatenate([wave * cos, wave * sin], axis=1)
    at = lax.broadcasted_iota(jnp.int32, (8, LANES), 0)
    tile = jnp.zeros((8, LANES), F32)
    for i in range(2):
        tile = jnp.where(at == 2 * i, waves[i:i + 1], tile)
        tile = jnp.where(at == 2 * i + 1, echo_ref[i:i + 1, :], tile)
    out_ref[...] = jnp.broadcast_to(tile[None], out_ref.shape)
    shown = shown_ref[...].astype(F32)
    out_ref[:, 4:6, 0:TILES_DEV] = jnp.broadcast_to(shown[None], (32, 2, TILES_DEV))


def pack(sub, echoes, offset, gates, shown):
    vmem = pl.BlockSpec(memory_space=pltpu.VMEM)
    return pl.pallas_call(
        pack_kernel,
        out_shape=jax.ShapeDtypeStruct((32, 8, LANES), F32),
        in_specs=[pl.BlockSpec(memory_space=pltpu.SMEM)] + [pl.BlockSpec(memory_space=pltpu.HBM)] * 4,
        out_specs=vmem,
        scratch_shapes=[
            pltpu.VMEM((2, LANES), F32),
            pltpu.VMEM((1, 2), F32),
            pltpu.VMEM((2, FREQS), jnp.int32),
            pltpu.VMEM((2, TILES_DEV), jnp.int32),
            pltpu.SemaphoreType.DMA((4,)),
        ],
    )(sub, echoes, offset, gates, shown)


def row(ref, at):
    return jnp.broadcast_to(ref[pl.ds(at, 1), :], (8, LANES))


def steps(tile_ref, sub_ref, g_ref, next_ref, sides, wave_ref, table_ref, prods, images_ref, out_ref, power_ref, sems,
          keep_ref=None, send_ref=None):
    tile_index = tile_ref[0]
    core = sub_ref[0] % 2 if sub_ref is not None else None
    x_first = ((tile_index % 2) * 1024 - 1024).astype(F32)
    y_first = ((tile_index // 2) * 128 - 512).astype(F32)
    scale = F32((2.0 * PULSE_H * FREQS) ** -0.5)
    low = lax.broadcasted_iota(jnp.int32, (16, LANES), 1) < FREQS
    sigma = lax.broadcasted_iota(jnp.int32, (8, LANES), 0).astype(F32) - 3.5
    backwards = 7 - lax.broadcasted_iota(jnp.int32, (8, LANES), 0)

    def halved(ref, at):
        m = ref[pl.ds(at, 32, stride=8), :]
        t = pltpu.roll(m, FREQS, 1)
        return jnp.where(low, m[:16], t[16:]), jnp.where(low, t[:16], m[16:])

    def tables(half):
        ref, at = (g_ref, 2 * half) if half < 2 else (next_ref, 0)
        ca, sa = halved(ref, at)
        er, ei = halved(ref, at + 1)
        wave_ref[0:16, :] = ca
        wave_ref[16:32, :] = sa

        def put(slot, v):
            table_ref[slot * 32: slot * 32 + 16, :] = v[0]
            table_ref[slot * 32 + 16: slot * 32 + 32, :] = v[1]

        e4 = sincos(ca * 4.0)
        e8 = times(e4, e4)
        v = e4
        for m in range(4):
            put(m, v)
            if m < 3:
                v = times(v, e8)
        e32 = times(v, e4)
        e64 = times(e32, e32)
        v = e32
        for j in range(4):
            put(4 + j, v)
            if j < 3:
                v = times(v, e64)
        e4 = sincos(sa * 4.0)
        e8 = times(e4, e4)
        v = e4
        for m in range(8):
            put(8 + m, v)
            if m < 7:
                v = times(v, e8)
        for block in range(2):
            phase = ca * (x_first + (255.5 + 512.0 * block)) + sa * (y_first + 63.5)
            put(16 + block, times((er * scale, ei * scale), sincos(phase)))

    def chunk(c, left_ref, right_ref):
        def entry(slot):
            return row(table_ref, slot * 32 + c), row(table_ref, slot * 32 + 16 + c)

        w = sincos(row(wave_ref, c) * sigma)
        for j in range(4):
            a = times(w, entry(4 + j))
            for m in (0, 2):
                near, far = turned_both(a, entry(m)), turned_both(a, entry(m + 1))
                for b, rows in ((4 + m, (near[0], far[0])), (2 - m, (far[1], near[1]))):
                    at = j * 64 + b * 8
                    for part in range(2):
                        left_ref[c, part * DEPTH + at: part * DEPTH + at + 16, :] = jnp.concatenate(
                            [rows[0][part], rows[1][part]], axis=0).astype(BF16)
        v = sincos(row(wave_ref, 16 + c) * sigma)
        for block in range(2):
            a = times(v, entry(16 + block))
            for m in (0, 2, 4, 6):
                near, far = turned_both(a, entry(8 + m)), turned_both(a, entry(9 + m))
                for b, rows in ((8 + m, (near[0], far[0])), (6 - m, (far[1], near[1]))):
                    at = block * 256 + b * 8
                    for part in range(2):
                        right_ref[c, part * 128 + at: part * 128 + at + 16, :] = jnp.concatenate(
                            [rows[0][part], rows[1][part]], axis=0).astype(BF16)

    def product(left_ref, right_ref, rows, columns):
        left = jnp.concatenate([left_ref[c, rows, :] for c in range(CHUNKS)], axis=1)
        right = jnp.concatenate([right_ref[c, columns, :] for c in range(CHUNKS)], axis=1)
        return lax.dot_general(left, right, (((1,), (1,)), ((), ())), preferred_element_type=F32)

    def stage(done, made):
        tables(made)
        if done is None:
            lax.fori_loop(0, CHUNKS, lambda c, carry: (chunk(c, *sides[made % 2]), carry)[1], 0)
        else:
            def step(i, carry):
                rows, columns = pl.ds(0, 512), pl.ds(pl.multiple_of(i * 256, 256), 256)
                prods[done][rows, columns] = product(*sides[done % 2], rows, columns)
                for c in range(8):
                    chunk(i * 8 + c, *sides[made % 2])
                return carry

            lax.fori_loop(0, 2, step, 0)

    def flip(v):
        return jnp.take_along_axis(v, backwards, axis=0)

    def weight(half, tile):
        ref, at = (g_ref, 4 + half) if half < 2 else (next_ref, 4)
        own = ref[pl.ds(tile_index * 8 + at, 1), :]
        return jnp.broadcast_to(own[:, tile:tile + 1], (8, LANES))

    def out_copy(s, tile):
        return pltpu.make_async_copy(out_ref.at[tile], images_ref.at[s, tile], sems.at[tile])

    def finish(s, block):
        for quarter in range(2):
            upper, lower = block * 4 + 2 + quarter, block * 4 + 1 - quarter
            up = [weight(half, upper) for half in (s, s + 1)]
            down = [weight(half, lower) for half in (s, s + 1)]
            for z in range(8):
                power_up, power_down = [], []
                for r in (2 * z, 2 * z + 1):
                    near = slice(quarter * 128 + r * 8, quarter * 128 + r * 8 + 8)
                    far = slice(DEPTH + near.start, DEPTH + near.stop)
                    above, below = [], []
                    for i in range(2):
                        pr = prods[s + i][near, block * 256: block * 256 + 128]
                        pi = prods[s + i][near, block * 256 + 128: block * 256 + 256]
                        qr = prods[s + i][far, block * 256: block * 256 + 128]
                        qi = prods[s + i][far, block * 256 + 128: block * 256 + 256]
                        above.append(((pr - qi) * up[i], (pi + qr) * up[i]))
                        below.append(((pr + qi) * down[i], (pi - qr) * down[i]))
                    for sums, tile, at, power, turn in ((above, upper, r, power_up, False),
                                                        (below, lower, 15 - r, power_down, True)):
                        rows = slice(at * 8, at * 8 + 8)
                        re, im = (sums[0][part] + sums[1][part] for part in range(2))
                        if turn:
                            re, im = flip(re), flip(im)
                        out_ref[tile, rows, 0:128] = re
                        out_ref[tile, rows, 128:256] = im
                        now = re * re + im * im
                        if s == 0:
                            power_ref[tile, rows, :] = now
                        else:
                            power.append(jnp.maximum(power_ref[tile, rows, :], now))
                if s == 1:
                    keep_ref[z, upper] = jnp.where(core == 0, power_up[0], power_up[1])
                    send_ref[z, upper] = jnp.where(core == 0, power_up[1], power_up[0])
                    keep_ref[7 - z, lower] = jnp.where(core == 0, power_down[1], power_down[0])
                    send_ref[7 - z, lower] = jnp.where(core == 0, power_down[0], power_down[1])

    def leave(s, block):
        for tile in range(block * 4, block * 4 + 4):
            out_copy(s, tile).start()

    def last_product(half, block):
        columns = slice(block * 256, block * 256 + 256)
        prods[half][:, columns] = product(*sides[half % 2], slice(0, 2 * DEPTH), columns)

    return stage, last_product, finish, leave, out_copy


def first_kernel(tile_ref, g_ref, images_ref, second_ref, power_ref,
                 left_a, left_b, right_a, right_b, wave_ref, table_ref, prod_ref, out_ref, sems):
    stage, last_product, finish, leave, out_copy = steps(
        tile_ref, None, g_ref, None, ((left_a, right_a), (left_b, right_b)), wave_ref, table_ref,
        (prod_ref, second_ref), images_ref, out_ref, power_ref, sems)
    stage(None, 0)
    stage(0, 1)
    last_product(1, 0)
    last_product(1, 1)
    finish(0, 0)
    leave(0, 0)
    finish(0, 1)
    leave(0, 1)
    for tile in range(TILES_DEV):
        out_copy(0, tile).wait()


def second_kernel(tile_ref, sub_ref, g_ref, next_ref, second_ref, power_ref, before_ref, images_ref, keep_ref, send_ref,
                  left_ref, right_ref, wave_ref, table_ref, prod_ref, out_ref, sems):
    stage, last_product, finish, leave, out_copy = steps(
        tile_ref, sub_ref, g_ref, next_ref, ((left_ref, right_ref),), wave_ref, table_ref,
        (None, second_ref, prod_ref), images_ref, out_ref, power_ref, sems, keep_ref, send_ref)
    stage(None, 2)
    last_product(2, 0)
    last_product(2, 1)
    finish(1, 0)
    leave(1, 0)
    finish(1, 1)
    leave(1, 1)
    for tile in range(TILES_DEV):
        out_copy(1, tile).wait()


def scratch(sides):
    return [
        *[pltpu.VMEM((CHUNKS, 2 * DEPTH, LANES), BF16)] * sides,
        *[pltpu.VMEM((CHUNKS, 512, LANES), BF16)] * sides,
        pltpu.VMEM((32, LANES), F32),
        pltpu.VMEM((18 * 32, LANES), F32),
        pltpu.VMEM((2 * DEPTH, 512), F32),
        pltpu.VMEM((TILES_DEV, PIX, 2 * PIX), F32),
        pltpu.SemaphoreType.DMA((TILES_DEV,)),
    ]


def first(tile, gathered):
    vmem, smem, anywhere = (pl.BlockSpec(memory_space=space) for space in (pltpu.VMEM, pltpu.SMEM, pl.ANY))
    return pl.pallas_call(
        first_kernel,
        out_shape=(jax.ShapeDtypeStruct((2, TILES_DEV, PIX, 2 * PIX), F32),
                   jax.ShapeDtypeStruct((2 * DEPTH, 512), F32),
                   jax.ShapeDtypeStruct((TILES_DEV, PIX, PIX), F32)),
        in_specs=[smem, vmem],
        out_specs=(anywhere, vmem, vmem),
        scratch_shapes=scratch(2),
        cost_estimate=pl.CostEstimate(flops=2 * 2 * 512 * 512 * 2048, bytes_accessed=8 << 20, transcendentals=0),
        compiler_params=pltpu.CompilerParams(vmem_limit_bytes=32 * 1024 * 1024),
    )(tile, gathered)


def second(tile, sub, gathered, following, product, power, images):
    vmem, smem, anywhere = (pl.BlockSpec(memory_space=space) for space in (pltpu.VMEM, pltpu.SMEM, pl.ANY))
    piece = jax.ShapeDtypeStruct((8, TILES_DEV, 8, LANES), F32)
    return pl.pallas_call(
        second_kernel,
        out_shape=(jax.ShapeDtypeStruct((2, TILES_DEV, PIX, 2 * PIX), F32), piece, piece),
        in_specs=[smem, smem, vmem, vmem, vmem, vmem, anywhere],
        out_specs=(anywhere, vmem, vmem),
        scratch_shapes=scratch(1),
        input_output_aliases={6: 0},
        compiler_params=pltpu.CompilerParams(vmem_limit_bytes=32 * 1024 * 1024),
    )(tile, sub, gathered, following, product, power, images)


def on_device(echoes, pulse_offset, range_gates, visible):
    sub = lax.axis_index("sub").astype(jnp.int32)[None]
    tile = lax.axis_index("tile").astype(jnp.int32)[None]
    subs = lax.axis_size("sub")
    own = pack(sub, echoes[:, 0], pulse_offset.reshape(1, 2), range_gates[:, 0], visible)
    gathered = lax.all_to_all(own, "tile", 0, 0, tiled=True).reshape(256, LANES)
    following = lax.ppermute(gathered, "sub", [((i + 1) % subs, i) for i in range(subs)])
    images, product, power = first(tile, gathered)
    images, keep, send = second(tile, sub, gathered, following, product, power, images)
    other = lax.ppermute(send, "sub", [(i, i ^ 1) for i in range(subs)])
    both = jnp.maximum(keep, other)
    groups = [[2 * z + c for z in range(subs // 2)] for c in range(2)]
    pieces = lax.all_to_all(both, "sub", 0, 0, tiled=True, axis_index_groups=groups)
    return images, jnp.max(pieces, axis=0)


def solution(mesh):
    in_specs = (P("sub", "tile", None), P("sub", "tile"), P("sub", "tile", None), P("sub", "tile"))
    out_specs = (P("sub", "tile", None, None), P("tile", "sub", None))
    return jax.shard_map(
        on_device, mesh=mesh, in_specs=in_specs, out_specs=out_specs, check_vma=False
    )
```

```python
import functools
import math

import jax
import jax.numpy as jnp
from jax import lax
from jax.experimental import pallas as pl
from jax.experimental.pallas import tpu as pltpu
from jax.sharding import PartitionSpec as P

PULSE_H = 32
FREQS = 64
PIX = 128
GATES = 512
LANES = 128
CHUNKS = PULSE_H * FREQS // LANES
TILES_DEV = 8
DEPTH = 256

two_pi = 2.0 * math.pi
F32 = jnp.float32
BF16 = jnp.bfloat16


def sincos(x):
    n = jnp.round(x * F32(2.0 / math.pi))
    r = ((x - n * F32(1.5703125)) - n * F32(4.837512969970703125e-4)) - n * F32(7.54978995489188216e-8)
    r2 = r * r
    s = r + r * r2 * (F32(-1.6666654611e-1) + r2 * (F32(8.3321608736e-3) + r2 * F32(-1.9515295891e-4)))
    c = (1.0 - 0.5 * r2) + r2 * r2 * (F32(4.166664568298827e-2) + r2 * (F32(-1.388731625493765e-3) + r2 * F32(2.443315711809948e-5)))
    q = n.astype(jnp.int32)
    odd = (q & 1) == 1
    cos = jnp.where(odd, s, c)
    sin = jnp.where(odd, c, s)
    cos = jnp.where(((q + 1) & 2) == 2, -cos, cos)
    sin = jnp.where((q & 2) == 2, -sin, sin)
    return cos, sin


def times(a, b):
    return a[0] * b[0] - a[1] * b[1], a[0] * b[1] + a[1] * b[0]


def turned_both(a, b):
    p, q, r, t = a[0] * b[0], a[1] * b[1], a[1] * b[0], a[0] * b[1]
    return (p - q, r + t), (p + q, r - t)


def pack_kernel(sub_ref, echo_hbm, offset_hbm, gates_hbm, shown_hbm, out_ref,
                echo_ref, offset_ref, gates_ref, shown_ref, sems):
    copies = [pltpu.make_async_copy(src, dst, sems.at[i]) for i, (src, dst) in enumerate((
        (echo_hbm, echo_ref), (offset_hbm, offset_ref), (gates_hbm, gates_ref), (shown_hbm, shown_ref)))]
    for copy in copies:
        copy.start()
    for copy in copies:
        copy.wait()
    first = lax.broadcasted_iota(jnp.int32, (2, FREQS), 0)
    half = (2 * sub_ref[0] + first).astype(F32)
    offset = jnp.where(first == 0, offset_ref[0:1, 0:1], offset_ref[0:1, 1:2])
    angle = two_pi * (half + offset) / 32
    wave = 0.5 + gates_ref[...].astype(F32) / GATES
    cos, sin = sincos(angle)
    waves = jnp.concatenate([wave * cos, wave * sin], axis=1)
    at = lax.broadcasted_iota(jnp.int32, (8, LANES), 0)
    tile = jnp.zeros((8, LANES), F32)
    for i in range(2):
        tile = jnp.where(at == 2 * i, waves[i:i + 1], tile)
        tile = jnp.where(at == 2 * i + 1, echo_ref[i:i + 1, :], tile)
    out_ref[...] = jnp.broadcast_to(tile[None], out_ref.shape)
    shown = shown_ref[...].astype(F32)
    out_ref[:, 4:6, 0:TILES_DEV] = jnp.broadcast_to(shown[None], (32, 2, TILES_DEV))


def pack(sub, echoes, offset, gates, shown):
    vmem = pl.BlockSpec(memory_space=pltpu.VMEM)
    return pl.pallas_call(
        pack_kernel,
        out_shape=jax.ShapeDtypeStruct((32, 8, LANES), F32),
        in_specs=[pl.BlockSpec(memory_space=pltpu.SMEM)] + [pl.BlockSpec(memory_space=pltpu.HBM)] * 4,
        out_specs=vmem,
        scratch_shapes=[
            pltpu.VMEM((2, LANES), F32),
            pltpu.VMEM((1, 2), F32),
            pltpu.VMEM((2, FREQS), jnp.int32),
            pltpu.VMEM((2, TILES_DEV), jnp.int32),
            pltpu.SemaphoreType.DMA((4,)),
        ],
    )(sub, echoes, offset, gates, shown)


def row(ref, at):
    return jnp.broadcast_to(ref[pl.ds(at, 1), :], (8, LANES))


def steps(tile_ref, sub_ref, g_ref, next_ref, sides, wave_ref, table_ref, prods, images_ref, out_ref, power_ref, sems,
          keep_ref=None, send_ref=None):
    tile_index = tile_ref[0]
    core = sub_ref[0] % 2 if sub_ref is not None else None
    x_first = ((tile_index % 2) * 1024 - 1024).astype(F32)
    y_first = ((tile_index // 2) * 128 - 512).astype(F32)
    scale = F32((2.0 * PULSE_H * FREQS) ** -0.5)
    low = lax.broadcasted_iota(jnp.int32, (16, LANES), 1) < FREQS
    sigma = lax.broadcasted_iota(jnp.int32, (8, LANES), 0).astype(F32) - 3.5
    backwards = 7 - lax.broadcasted_iota(jnp.int32, (8, LANES), 0)

    def halved(ref, at):
        m = ref[pl.ds(at, 32, stride=8), :]
        t = pltpu.roll(m, FREQS, 1)
        return jnp.where(low, m[:16], t[16:]), jnp.where(low, t[:16], m[16:])

    def tables(half):
        ref, at = (g_ref, 2 * half) if half < 2 else (next_ref, 0)
        ca, sa = halved(ref, at)
        er, ei = halved(ref, at + 1)
        wave_ref[0:16, :] = ca
        wave_ref[16:32, :] = sa

        def put(slot, v):
            table_ref[slot * 32: slot * 32 + 16, :] = v[0]
            table_ref[slot * 32 + 16: slot * 32 + 32, :] = v[1]

        e4 = sincos(ca * 4.0)
        e8 = times(e4, e4)
        v = e4
        for m in range(4):
            put(m, v)
            if m < 3:
                v = times(v, e8)
        e32 = times(v, e4)
        e64 = times(e32, e32)
        v = e32
        for j in range(4):
            put(4 + j, v)
            if j < 3:
                v = times(v, e64)
        e4 = sincos(sa * 4.0)
        e8 = times(e4, e4)
        v = e4
        for m in range(8):
            put(8 + m, v)
            if m < 7:
                v = times(v, e8)
        for block in range(2):
            phase = ca * (x_first + (255.5 + 512.0 * block)) + sa * (y_first + 63.5)
            put(16 + block, times((er * scale, ei * scale), sincos(phase)))

    def chunk(c, left_ref, right_ref):
        def entry(slot):
            return row(table_ref, slot * 32 + c), row(table_ref, slot * 32 + 16 + c)

        w = sincos(row(wave_ref, c) * sigma)
        for j in range(4):
            a = times(w, entry(4 + j))
            for m in (0, 2):
                near, far = turned_both(a, entry(m)), turned_both(a, entry(m + 1))
                for b, rows in ((4 + m, (near[0], far[0])), (2 - m, (far[1], near[1]))):
                    at = j * 64 + b * 8
                    for part in range(2):
                        left_ref[c, part * DEPTH + at: part * DEPTH + at + 16, :] = jnp.concatenate(
                            [rows[0][part], rows[1][part]], axis=0).astype(BF16)
        v = sincos(row(wave_ref, 16 + c) * sigma)
        for block in range(2):
            a = times(v, entry(16 + block))
            for m in (0, 2, 4, 6):
                near, far = turned_both(a, entry(8 + m)), turned_both(a, entry(9 + m))
                for b, rows in ((8 + m, (near[0], far[0])), (6 - m, (far[1], near[1]))):
                    at = block * 256 + b * 8
                    for part in range(2):
                        right_ref[c, part * 128 + at: part * 128 + at + 16, :] = jnp.concatenate(
                            [rows[0][part], rows[1][part]], axis=0).astype(BF16)

    def product(left_ref, right_ref, rows, columns):
        left = jnp.concatenate([left_ref[c, rows, :] for c in range(CHUNKS)], axis=1)
        right = jnp.concatenate([right_ref[c, columns, :] for c in range(CHUNKS)], axis=1)
        return lax.dot_general(left, right, (((1,), (1,)), ((), ())), preferred_element_type=F32)

    def stage(done, made):
        tables(made)
        if done is None:
            lax.fori_loop(0, CHUNKS, lambda c, carry: (chunk(c, *sides[made % 2]), carry)[1], 0)
        else:
            def step(i, carry):
                rows, columns = pl.ds(0, 512), pl.ds(pl.multiple_of(i * 256, 256), 256)
                prods[done][rows, columns] = product(*sides[done % 2], rows, columns)
                for c in range(8):
                    chunk(i * 8 + c, *sides[made % 2])
                return carry

            lax.fori_loop(0, 2, step, 0)

    def flip(v):
        return jnp.take_along_axis(v, backwards, axis=0)

    def weight(half, tile):
        ref, at = (g_ref, 4 + half) if half < 2 else (next_ref, 4)
        own = ref[pl.ds(tile_index * 8 + at, 1), :]
        return jnp.broadcast_to(own[:, tile:tile + 1], (8, LANES))

    def out_copy(tile):
        return pltpu.make_async_copy(out_ref.at[tile], images_ref.at[1, tile], sems.at[tile])

    def finish(s, block):
        for quarter in range(2):
            upper, lower = block * 4 + 2 + quarter, block * 4 + 1 - quarter
            up = [weight(half, upper) for half in (s, s + 1)]
            down = [weight(half, lower) for half in (s, s + 1)]
            for z in range(8):
                power_up, power_down = [], []
                for r in (2 * z, 2 * z + 1):
                    near = slice(quarter * 128 + r * 8, quarter * 128 + r * 8 + 8)
                    far = slice(DEPTH + near.start, DEPTH + near.stop)
                    above, below = [], []
                    for i in range(2):
                        pr = prods[s + i][near, block * 256: block * 256 + 128]
                        pi = prods[s + i][near, block * 256 + 128: block * 256 + 256]
                        qr = prods[s + i][far, block * 256: block * 256 + 128]
                        qi = prods[s + i][far, block * 256 + 128: block * 256 + 256]
                        above.append(((pr - qi) * up[i], (pi + qr) * up[i]))
                        below.append(((pr + qi) * down[i], (pi - qr) * down[i]))
                    for sums, tile, at, power, turn in ((above, upper, r, power_up, False),
                                                        (below, lower, 15 - r, power_down, True)):
                        rows = slice(at * 8, at * 8 + 8)
                        re, im = (sums[0][part] + sums[1][part] for part in range(2))
                        if turn:
                            re, im = flip(re), flip(im)
                        out_ref[tile, rows, 0:128] = re
                        out_ref[tile, rows, 128:256] = im
                        now = re * re + im * im
                        if s == 0:
                            power_ref[tile, rows, :] = now
                        else:
                            power.append(jnp.maximum(power_ref[tile, rows, :], now))
                if s == 1:
                    keep_ref[z, upper] = jnp.where(core == 0, power_up[0], power_up[1])
                    send_ref[z, upper] = jnp.where(core == 0, power_up[1], power_up[0])
                    keep_ref[7 - z, lower] = jnp.where(core == 0, power_down[1], power_down[0])
                    send_ref[7 - z, lower] = jnp.where(core == 0, power_down[0], power_down[1])
            if s == 1:
                out_copy(upper).start()
                out_copy(lower).start()

    def last_product(half, block):
        columns = slice(block * 256, block * 256 + 256)
        prods[half][:, columns] = product(*sides[half % 2], slice(0, 2 * DEPTH), columns)

    return stage, last_product, finish, out_copy


def first_kernel(tile_ref, g_ref, early_ref, second_ref, power_ref,
                 left_a, left_b, right_a, right_b, wave_ref, table_ref, prod_ref):
    stage, last_product, finish, _ = steps(
        tile_ref, None, g_ref, None, ((left_a, right_a), (left_b, right_b)), wave_ref, table_ref,
        (prod_ref, second_ref), None, early_ref, power_ref, None)
    stage(None, 0)
    stage(0, 1)
    last_product(1, 0)
    last_product(1, 1)
    finish(0, 0)
    finish(0, 1)


def second_kernel(tile_ref, sub_ref, g_ref, next_ref, second_ref, power_ref, early_ref, images_ref, keep_ref, send_ref,
                  left_ref, right_ref, wave_ref, table_ref, prod_ref, out_ref, sems):
    stage, last_product, finish, out_copy = steps(
        tile_ref, sub_ref, g_ref, next_ref, ((left_ref, right_ref),), wave_ref, table_ref,
        (None, second_ref, prod_ref), images_ref, out_ref, power_ref, sems, keep_ref, send_ref)
    early = pltpu.make_async_copy(early_ref, images_ref.at[0], sems.at[TILES_DEV])
    early.start()
    stage(None, 2)
    last_product(2, 0)
    last_product(2, 1)
    finish(1, 0)
    finish(1, 1)
    early.wait()
    for tile in range(TILES_DEV):
        out_copy(tile).wait()


def scratch(sides):
    return [
        *[pltpu.VMEM((CHUNKS, 2 * DEPTH, LANES), BF16)] * sides,
        *[pltpu.VMEM((CHUNKS, 512, LANES), BF16)] * sides,
        pltpu.VMEM((32, LANES), F32),
        pltpu.VMEM((18 * 32, LANES), F32),
        pltpu.VMEM((2 * DEPTH, 512), F32),
    ]


def first(tile, gathered):
    vmem, smem = (pl.BlockSpec(memory_space=space) for space in (pltpu.VMEM, pltpu.SMEM))
    return pl.pallas_call(
        first_kernel,
        out_shape=(jax.ShapeDtypeStruct((TILES_DEV, PIX, 2 * PIX), F32),
                   jax.ShapeDtypeStruct((2 * DEPTH, 512), F32),
                   jax.ShapeDtypeStruct((TILES_DEV, PIX, PIX), F32)),
        in_specs=[smem, vmem],
        out_specs=(vmem, vmem, vmem),
        scratch_shapes=scratch(2),
        cost_estimate=pl.CostEstimate(flops=2 * 2 * 512 * 512 * 2048, bytes_accessed=8 << 20, transcendentals=0),
        compiler_params=pltpu.CompilerParams(vmem_limit_bytes=32 * 1024 * 1024),
    )(tile, gathered)


def second(tile, sub, gathered, following, product, power, early):
    vmem, smem, anywhere = (pl.BlockSpec(memory_space=space) for space in (pltpu.VMEM, pltpu.SMEM, pl.ANY))
    piece = jax.ShapeDtypeStruct((8, TILES_DEV, 8, LANES), F32)
    return pl.pallas_call(
        second_kernel,
        out_shape=(jax.ShapeDtypeStruct((2, TILES_DEV, PIX, 2 * PIX), F32), piece, piece),
        in_specs=[smem, smem] + [vmem] * 5,
        out_specs=(anywhere, vmem, vmem),
        scratch_shapes=scratch(1) + [pltpu.VMEM((TILES_DEV, PIX, 2 * PIX), F32), pltpu.SemaphoreType.DMA((TILES_DEV + 1,))],
        compiler_params=pltpu.CompilerParams(vmem_limit_bytes=32 * 1024 * 1024),
    )(tile, sub, gathered, following, product, power, early)


def on_device(echoes, pulse_offset, range_gates, visible):
    sub = lax.axis_index("sub").astype(jnp.int32)[None]
    tile = lax.axis_index("tile").astype(jnp.int32)[None]
    subs = lax.axis_size("sub")
    own = pack(sub, echoes[:, 0], pulse_offset.reshape(1, 2), range_gates[:, 0], visible)
    gathered = lax.all_to_all(own, "tile", 0, 0, tiled=True).reshape(256, LANES)
    following = lax.ppermute(gathered, "sub", [((i + 1) % subs, i) for i in range(subs)])
    early, product, power = first(tile, gathered)
    images, keep, send = second(tile, sub, gathered, following, product, power, early)
    other = lax.ppermute(send, "sub", [(i, i ^ 1) for i in range(subs)])
    both = jnp.maximum(keep, other)
    groups = [[2 * z + c for z in range(subs // 2)] for c in range(2)]
    pieces = lax.all_to_all(both, "sub", 0, 0, tiled=True, axis_index_groups=groups)
    return images, jnp.max(pieces, axis=0)


def solution(mesh):
    in_specs = (P("sub", "tile", None), P("sub", "tile"), P("sub", "tile", None), P("sub", "tile"))
    out_specs = (P("sub", "tile", None, None), P("tile", "sub", None))
    return jax.shard_map(
        on_device, mesh=mesh, in_specs=in_specs, out_specs=out_specs, check_vma=False
    )
```
